32 devices in a mesh: node: 2 (over core), dp: 16 (over z, y, x).
Axes of the slice: x: 2, y: 2, z: 4, core: 2. Of those that a mesh axis runs over, the one named last changes fastest.
Arguments:
- hidden: bfloat16 [16, 256, 13824], P('dp', 'node'), may hold values from -6 to 6
- cotangent: bfloat16 [16, 256, 16], P('dp', 'node'), may hold values from -0.375 to 0.375
- momentum: float32 [16, 16, 13824], P('dp', 'node'), may hold values from -6 to 6
- worker_error: float32 [16, 16, 13824], P('dp', 'node'), may hold values from -1.8 to 1.8
- server_error: float32 [16, 13824], P('node', 'dp'), may hold values from -0.3 to 0.3
- master: float32 [16, 13824], P('node'), may hold values from -3 to 3
- second_moment: float32 [16, 13824], P('node'), may hold values from 0.0004 to 0.01
Outputs:
- moment: float32 [16, 16, 13824], P('dp', 'node')
- new_worker_error: float32 [16, 16, 13824], P('dp', 'node')
- new_server_error: float32 [16, 13824], P('node', 'dp')
- weights: bfloat16 [16, 13824], replicated
The draws below stay inside these ranges and needn't reach their ends.
All inputs are finite; a program needn't handle non-finite values.
Results may differ from the reference program's by a relative error of at most 0.0085.
Values may be sent and summed in bfloat16 or wider, within the bound.
No kernel may reach another device: no remote copies, remote signals or barrier semaphores. Data moves between devices by JAX's collectives and lax.ppermute only.
A program may use at most 64 MiB of HBM per device.

```python
import math
import jax
import jax.numpy as jnp
from jax import lax

FF = 13824
ROWS = 16
NODE_TOK = 256
REPLICAS = 16
N_NODE = 2
N_DP = 16


def steps_of(own_key, dims, cuts, smallest, high):
    def one(position, shards_of):
        steps = jax.random.uniform(jax.random.fold_in(jax.random.fold_in(own_key, 6), position), (shards_of,), jnp.float32, smallest / len(cuts), high / len(cuts))
        return jnp.repeat(jnp.exp(steps), dims[position] // shards_of).reshape((-1,) + (1,) * (len(dims) - position - 1))

    level = one(*cuts[0])
    for cut in cuts[1:]:
        level = level * one(*cut)
    return level


def noise(key, dims, width, limit, cuts=(), held_as=jnp.bfloat16):
    factor_of = steps_of(key, dims, cuts, -0.22, 0.18) if cuts else 1.0
    result = jax.random.normal(key, dims, jnp.float32) * width * factor_of
    return jnp.minimum(jnp.maximum(result, -limit), limit).astype(held_as)


def setup_inputs(seed: int = 0) -> dict:
    splits = jax.random.split(jax.random.key(seed), 8)
    return {
        "hidden": noise(splits[0], (REPLICAS, NODE_TOK, FF), 1.0, 6.0, ((0, 16), (1, 2))),
        "cotangent": noise(splits[1], (REPLICAS, NODE_TOK, ROWS), (1.0 / NODE_TOK ** 0.5), 0.375, ((0, 16), (1, 2))),
        "momentum": noise(splits[2], (REPLICAS, ROWS, FF), 1.0, 6.0, ((0, 16), (1, 2)), jnp.float32),
        "worker_error": noise(splits[3], (REPLICAS, ROWS, FF), 0.3, 1.8, ((0, 16), (1, 2)), jnp.float32),
        "server_error": noise(splits[4], (ROWS, FF), 0.05, 0.3, ((0, 2), (1, 16)), jnp.float32),
        "master": noise(splits[5], (ROWS, FF), 0.5, 3.0, ((0, 2),), jnp.float32),
        "second_moment": jnp.clip(jnp.exp(math.log(0.01) - 3.218876 * jax.random.uniform(splits[6], (ROWS, FF), jnp.float32) ** steps_of(splits[6], (ROWS, FF), ((0, 2),), -0.2, 0.2)), 0.0004, 0.01),
    }


beta_one = 0.9
epsilon = 1e-06
learn_rate = 0.5

def replica_gradient(pair):
    cotan, acts = pair
    return jnp.dot(cotan.T, acts, preferred_element_type=jnp.float32)

def reference(hidden, cotangent, momentum, worker_error, server_error, master, second_moment):
    gradient = lax.map(replica_gradient, (cotangent, hidden))
    moment = beta_one * momentum + (1.0 - beta_one) * gradient
    carried = moment + worker_error
    blocks = carried.reshape(N_DP, N_NODE, ROWS // N_NODE, FF)
    worker_scale = jnp.sqrt(lax.optimization_barrier(jnp.mean(blocks * blocks, axis=(2, 3), keepdims=True)) + epsilon)
    sent = (worker_scale * jnp.tanh(blocks / worker_scale)).astype(jnp.bfloat16)
    new_worker = (blocks - sent.astype(jnp.float32)).reshape(N_DP, ROWS, FF)
    average = lax.optimization_barrier(jnp.sum(sent.astype(jnp.float32), axis=0)) / N_DP
    served = average.reshape(ROWS, FF) + server_error
    pieces = served.reshape(N_NODE, ROWS // N_NODE, N_DP, FF // N_DP)
    server_scale = jnp.sqrt(lax.optimization_barrier(jnp.mean(pieces * pieces, axis=(1, 3), keepdims=True)) + epsilon)
    returned = (server_scale * jnp.tanh(pieces / server_scale)).astype(jnp.bfloat16)
    new_server = (pieces - returned.astype(jnp.float32)).reshape(ROWS, FF)
    update = returned.astype(jnp.float32).reshape(ROWS, FF) / (jnp.sqrt(second_moment) + 1e-08)
    weights = (master - learn_rate * update).astype(jnp.bfloat16)
    return (moment, new_worker, new_server, weights)
```

```python
import functools

import jax
import jax.numpy as jnp
from jax import lax
from jax.experimental import pallas as pl
from jax.experimental.pallas import tpu as pltpu
from jax.sharding import PartitionSpec as P

beta_one = 0.9
epsilon = 1e-06
learn_rate = 0.5
LANES = 128

VMEM = pl.BlockSpec(memory_space=pltpu.VMEM)
ANY = pl.BlockSpec(memory_space=pl.ANY)


def chunk_count(cols, most):
    if cols % LANES:
        return 1
    return max(n for n in range(1, most + 1) if (cols // LANES) % n == 0)


def gradient_kernel(cotan_ref, acts_hbm, mine_ref, theirs_ref, acts, sems):
    rows = cotan_ref.shape[0]
    own = mine_ref.shape[0]
    chunks = sems.shape[0]
    width = acts.shape[1] // chunks
    spans = [pl.ds(i * width, width) for i in range(chunks)]
    copies = [pltpu.make_async_copy(acts_hbm.at[:, s], acts.at[:, s], sems.at[i]) for i, s in enumerate(spans)]
    for copy in copies:
        copy.start()
    shift = lax.rem(rows - lax.axis_index("node") * own, rows)
    cotan = pltpu.roll(cotan_ref[...].astype(jnp.float32), shift, 0).astype(jnp.bfloat16)
    for copy, s in zip(copies, spans):
        copy.wait()
        sums = jnp.dot(cotan, acts[:, s], preferred_element_type=jnp.float32)
        mine_ref[:, s] = sums[:own]
        for k in range(theirs_ref.shape[0]):
            theirs_ref[k, :, s] = sums[(k + 1) * own : (k + 2) * own]


def moment_of(momentum_ref, mine_ref, arrived_refs):
    gradient = mine_ref[...]
    for ref in arrived_refs:
        gradient = gradient + ref[...]
    return beta_one * momentum_ref[...] + (1.0 - beta_one) * gradient


def compress(values):
    scale = jnp.sqrt(jnp.mean(values * values, keepdims=True) + epsilon)
    return (scale * jnp.tanh(values / scale)).astype(jnp.bfloat16)


def send_kernel(momentum_ref, error_ref, mine_ref, *refs):
    arrived_refs, (blocks_ref, carried_ref, sent_ref) = refs[:-3], refs[-3:]
    carried = moment_of(momentum_ref, mine_ref, arrived_refs) + error_ref[...]
    carried_ref[...] = carried
    sent = compress(carried)
    sent_ref[...] = sent
    width = blocks_ref.shape[2]
    for i in range(blocks_ref.shape[0]):
        blocks_ref[i] = sent[:, i * width : (i + 1) * width]


def keep_kernel(momentum_ref, carried_ref, sent_ref, master_hbm, second_hbm, mine_ref, *refs):
    arrived_refs = refs[:-7]
    moment_ref, error_ref, master_ref, bottom_ref, window, sem_a, sem_b = refs[-7:]
    width, span, cols = master_ref.shape[1], window.shape[2], master_hbm.shape[1]
    column = lax.axis_index("dp") * width
    start = jnp.minimum((column // LANES) * LANES, cols - span)
    here = pl.ds(pl.multiple_of(start, LANES), span)
    copy_a = pltpu.make_async_copy(master_hbm.at[:, here], window.at[0], sem_a)
    copy_b = pltpu.make_async_copy(second_hbm.at[:, here], window.at[1], sem_b)
    copy_a.start()
    copy_b.start()
    moment_ref[...] = moment_of(momentum_ref, mine_ref, arrived_refs)
    error_ref[...] = carried_ref[...] - sent_ref[...].astype(jnp.float32)
    shift = lax.rem(span - (column - start), span)
    copy_a.wait()
    copy_b.wait()
    master_ref[...] = pltpu.roll(window[0], shift, 1)[:, :width]
    bottom_ref[...] = jnp.sqrt(pltpu.roll(window[1], shift, 1)[:, :width]) + 1e-08


def serve_kernel(blocks_ref, error_ref, master_ref, bottom_ref, new_error_ref, out_ref):
    replicas = blocks_ref.shape[0]
    total = blocks_ref[0].astype(jnp.float32)
    for i in range(1, replicas):
        total = total + blocks_ref[i].astype(jnp.float32)
    served = total / replicas + error_ref[...]
    returned = compress(served).astype(jnp.float32)
    new_error_ref[...] = served - returned
    weights = (master_ref[...] - learn_rate * (returned / bottom_ref[...])).astype(jnp.bfloat16)
    for i in range(replicas):
        out_ref[i] = weights


def assemble_kernel(*refs):
    parts, out_ref = refs[:-1], refs[-1]
    nodes = len(parts)
    servers, own, width = parts[0].shape
    me = lax.axis_index("node")
    for i in range(servers):
        loaded = [part[i].astype(jnp.float32) for part in parts]
        stacked = []
        for node in range(nodes):
            chosen = loaded[0]
            for k in range(1, nodes):
                chosen = jnp.where(lax.rem(me - k + nodes, nodes) == node, loaded[k], chosen)
            stacked.append(chosen)
        out_ref[:, i * width : (i + 1) * width] = jnp.concatenate(stacked, axis=0).astype(jnp.bfloat16)


def body(hidden, cotangent, momentum, worker_error, server_error, master, second_moment):
    f32, bf16 = jnp.float32, jnp.bfloat16
    nodes, servers = lax.axis_size("node"), lax.axis_size("dp")
    tokens, cols = hidden.shape[1:]
    rows, own = cotangent.shape[2], momentum.shape[1]
    width = cols // servers
    shape = jax.ShapeDtypeStruct

    def turn(value, k):
        return lax.ppermute(value, "node", [(i, (i + k) % nodes) for i in range(nodes)])

    chunks = chunk_count(cols, 6)
    mine, theirs = pl.pallas_call(
        gradient_kernel,
        name="gradient",
        out_shape=(shape((own, cols), f32), shape((nodes - 1, own, cols), f32)),
        in_specs=[VMEM, ANY],
        out_specs=(VMEM, VMEM),
        scratch_shapes=[pltpu.VMEM((tokens, cols), bf16), pltpu.SemaphoreType.DMA((chunks,))],
    )(cotangent[0].T, hidden[0])
    arrived = [turn(theirs[k - 1], k) for k in range(1, nodes)]

    blocks, carried, sent = pl.pallas_call(
        send_kernel,
        name="send",
        out_shape=(shape((servers, own, width), bf16), shape((own, cols), f32), shape((own, cols), bf16)),
        in_specs=[VMEM] * (3 + len(arrived)),
        out_specs=(VMEM, VMEM, VMEM),
    )(momentum[0], worker_error[0], mine, *arrived)
    gathered = lax.all_to_all(blocks, "dp", split_axis=0, concat_axis=0, tiled=True)

    span = min(cols, -(-width // LANES) * LANES + LANES)
    moment, new_worker, master_part, bottom = pl.pallas_call(
        keep_kernel,
        name="keep",
        out_shape=(shape((own, cols), f32), shape((own, cols), f32), shape((own, width), f32), shape((own, width), f32)),
        in_specs=[VMEM, VMEM, VMEM, ANY, ANY] + [VMEM] * (1 + len(arrived)),
        out_specs=(VMEM, VMEM, VMEM, VMEM),
        scratch_shapes=[pltpu.VMEM((2, own, span), f32), pltpu.SemaphoreType.DMA(()), pltpu.SemaphoreType.DMA(())],
    )(momentum[0], carried, sent, master, second_moment, mine, *arrived)

    new_server, copies = pl.pallas_call(
        serve_kernel,
        name="serve",
        out_shape=(shape((own, width), f32), shape((servers, own, width), bf16)),
        in_specs=[VMEM] * 4,
        out_specs=(VMEM, VMEM),
    )(gathered, server_error, master_part, bottom)
    everyone = lax.all_to_all(copies, "dp", split_axis=0, concat_axis=0, tiled=True)
    parts = [everyone] + [turn(everyone, k) for k in range(1, nodes)]

    weights = pl.pallas_call(
        assemble_kernel,
        name="assemble",
        out_shape=shape((rows, cols), bf16),
        in_specs=[VMEM] * nodes,
        out_specs=VMEM,
    )(*parts)
    return (moment[None], new_worker[None], new_server, weights)


def solution(mesh):
    placed = (
        P("dp", "node", None),
        P("dp", "node", None),
        P("dp", "node", None),
        P("dp", "node", None),
        P("node", "dp"),
        P("node", None),
        P("node", None),
    )
    return jax.shard_map(
        body,
        mesh=mesh,
        in_specs=placed,
        out_specs=(P("dp", "node", None), P("dp", "node", None), P("node", "dp"), P()),
        check_vma=False,
    )
```

```python
import functools

import jax
import jax.numpy as jnp
from jax import lax
from jax.experimental import pallas as pl
from jax.experimental.pallas import tpu as pltpu
from jax.sharding import PartitionSpec as P

beta_one = 0.9
epsilon = 1e-06
learn_rate = 0.5
LANES = 128

VMEM = pl.BlockSpec(memory_space=pltpu.VMEM)
HBM = pl.BlockSpec(memory_space=pltpu.HBM)
MIB = 2**20


def near(*values):
    return [pltpu.with_memory_space_constraint(v, pltpu.VMEM) for v in values]


def far(*values):
    return [pltpu.with_memory_space_constraint(v, pltpu.HBM) for v in values]


def chunk_count(cols, most):
    if cols % LANES:
        return 1
    return max(n for n in range(1, most + 1) if (cols // LANES) % n == 0)


def gradient_kernel(cotan_hbm, momentum_hbm, acts_hbm, base_ref, theirs_ref, cotan_ref, acts, sems, cotan_sem, base_sem):
    rows = cotan_ref.shape[0]
    own = base_ref.shape[0]
    chunks = sems.shape[0]
    width = acts.shape[1] // chunks
    spans = [pl.ds(i * width, width) for i in range(chunks)]
    cotan_copy = pltpu.make_async_copy(cotan_hbm, cotan_ref, cotan_sem)
    base_copy = pltpu.make_async_copy(momentum_hbm, base_ref, base_sem)
    copies = [pltpu.make_async_copy(acts_hbm.at[:, s], acts.at[:, s], sems.at[i]) for i, s in enumerate(spans)]
    cotan_copy.start()
    copies[0].start()
    base_copy.start()
    for copy in copies[1:]:
        copy.start()
    shift = lax.rem(rows - lax.axis_index("node") * own, rows)
    cotan_copy.wait()
    cotan = pltpu.roll(cotan_ref[...].astype(jnp.float32), shift, 0).astype(jnp.bfloat16)
    for i, (copy, s) in enumerate(zip(copies, spans)):
        copy.wait()
        if i == 0:
            base_copy.wait()
        sums = jnp.dot(cotan, acts[:, s], preferred_element_type=jnp.float32)
        base_ref[:, s] = beta_one * base_ref[:, s] + (1.0 - beta_one) * sums[:own]
        for k in range(theirs_ref.shape[0]):
            theirs_ref[k, :, s] = sums[(k + 1) * own : (k + 2) * own]


def moment_of(base_ref, arrived_refs):
    rest = arrived_refs[0][...]
    for ref in arrived_refs[1:]:
        rest = rest + ref[...]
    return base_ref[...] + (1.0 - beta_one) * rest


def compress(values):
    scale = jnp.sqrt(jnp.mean(values * values, keepdims=True) + epsilon)
    return (scale * jnp.tanh(values / scale)).astype(jnp.bfloat16)


def send_kernel(error_ref, base_ref, *refs):
    arrived_refs, (blocks_ref, carried_ref, sent_ref) = refs[:-3], refs[-3:]
    carried = moment_of(base_ref, arrived_refs) + error_ref[...]
    carried_ref[...] = carried
    sent = compress(carried)
    sent_ref[...] = sent
    width = blocks_ref.shape[2]
    for i in range(blocks_ref.shape[0]):
        blocks_ref[i] = sent[:, i * width : (i + 1) * width]


def keep_kernel(carried_ref, sent_ref, master_hbm, second_hbm, base_ref, *refs):
    arrived_refs = refs[:-7]
    moment_ref, error_ref, master_ref, bottom_ref, window, sem_a, sem_b = refs[-7:]
    width, span, cols = master_ref.shape[1], window.shape[2], master_hbm.shape[1]
    column = lax.axis_index("dp") * width
    start = jnp.minimum((column // LANES) * LANES, cols - span)
    here = pl.ds(pl.multiple_of(start, LANES), span)
    copy_a = pltpu.make_async_copy(master_hbm.at[:, here], window.at[0], sem_a)
    copy_b = pltpu.make_async_copy(second_hbm.at[:, here], window.at[1], sem_b)
    copy_a.start()
    copy_b.start()
    moment_ref[...] = moment_of(base_ref, arrived_refs)
    error_ref[...] = carried_ref[...] - sent_ref[...].astype(jnp.float32)
    shift = lax.rem(span - (column - start), span)
    copy_a.wait()
    copy_b.wait()
    master_ref[...] = pltpu.roll(window[0], shift, 1)[:, :width]
    bottom_ref[...] = jnp.sqrt(pltpu.roll(window[1], shift, 1)[:, :width]) + 1e-08


def serve_kernel(blocks_ref, error_ref, master_ref, bottom_ref, new_error_ref, out_ref):
    replicas = blocks_ref.shape[0]
    total = blocks_ref[0].astype(jnp.float32)
    for i in range(1, replicas):
        total = total + blocks_ref[i].astype(jnp.float32)
    served = total / replicas + error_ref[...]
    returned = compress(served).astype(jnp.float32)
    new_error_ref[...] = served - returned
    weights = (master_ref[...] - learn_rate * (returned / bottom_ref[...])).astype(jnp.bfloat16)
    for i in range(replicas):
        out_ref[i] = weights


def assemble_kernel(*refs):
    parts, out_ref = refs[:-1], refs[-1]
    nodes = len(parts)
    servers, own, width = parts[0].shape
    me = lax.axis_index("node")
    for i in range(servers):
        loaded = [part[i].astype(jnp.float32) for part in parts]
        stacked = []
        for node in range(nodes):
            chosen = loaded[0]
            for k in range(1, nodes):
                chosen = jnp.where(lax.rem(me - k + nodes, nodes) == node, loaded[k], chosen)
            stacked.append(chosen)
        out_ref[:, i * width : (i + 1) * width] = jnp.concatenate(stacked, axis=0).astype(jnp.bfloat16)


def body(hidden, cotangent, momentum, worker_error, server_error, master, second_moment):
    f32, bf16 = jnp.float32, jnp.bfloat16
    nodes, servers = lax.axis_size("node"), lax.axis_size("dp")
    tokens, cols = hidden.shape[1:]
    rows, own = cotangent.shape[2], momentum.shape[1]
    width = cols // servers
    shape = jax.ShapeDtypeStruct

    def turn(value, k):
        return lax.ppermute(value, "node", [(i, (i + k) % nodes) for i in range(nodes)])

    def call(kernel, name, outs, specs, scratch=(), limit=16 * MIB):
        return pl.pallas_call(
            kernel,
            name=name,
            out_shape=outs,
            in_specs=specs,
            out_specs=jax.tree.map(lambda _: VMEM, outs),
            scratch_shapes=scratch,
            compiler_params=pltpu.CompilerParams(vmem_limit_bytes=limit),
        )

    chunks = chunk_count(cols, 6)
    base, theirs = call(
        gradient_kernel,
        "gradient",
        (pltpu.VMEM((own, cols), f32), pltpu.VMEM((nodes - 1, own, cols), f32)),
        [HBM] * 3,
        [pltpu.VMEM((rows, tokens), bf16), pltpu.VMEM((tokens, cols), bf16), pltpu.SemaphoreType.DMA((chunks,))]
        + [pltpu.SemaphoreType.DMA(())] * 2,
    )(*far(cotangent[0].T, momentum[0], hidden[0]))
    arrived = [turn(theirs[k - 1], k) for k in range(1, nodes)]

    blocks, carried, sent = call(
        send_kernel,
        "send",
        (pltpu.VMEM((servers, own, width), bf16), pltpu.VMEM((own, cols), f32), pltpu.VMEM((own, cols), bf16)),
        [VMEM] * (2 + len(arrived)),
    )(*near(worker_error[0], base, *arrived))
    gathered = lax.all_to_all(blocks, "dp", split_axis=0, concat_axis=0, tiled=True)

    span = min(cols, -(-width // LANES) * LANES + LANES)
    moment, new_worker, master_part, bottom = call(
        keep_kernel,
        "keep",
        (shape((own, cols), f32), shape((own, cols), f32), pltpu.VMEM((own, width), f32), pltpu.VMEM((own, width), f32)),
        [VMEM, VMEM, HBM, HBM] + [VMEM] * (1 + len(arrived)),
        [pltpu.VMEM((2, own, span), f32), pltpu.SemaphoreType.DMA(()), pltpu.SemaphoreType.DMA(())],
    )(*near(carried, sent), *far(master, second_moment), *near(base, *arrived))

    new_server, copies = call(
        serve_kernel,
        "serve",
        (shape((own, width), f32), pltpu.VMEM((servers, own, width), bf16)),
        [VMEM] * 4,
    )(*near(gathered, server_error, master_part, bottom))
    everyone = lax.all_to_all(copies, "dp", split_axis=0, concat_axis=0, tiled=True)
    parts = [everyone] + [turn(everyone, k) for k in range(1, nodes)]

    weights = call(assemble_kernel, "assemble", shape((rows, cols), bf16), [VMEM] * nodes)(*near(*parts))
    return (moment[None], new_worker[None], new_server, weights)


def solution(mesh):
    placed = (
        P("dp", "node", None),
        P("dp", "node", None),
        P("dp", "node", None),
        P("dp", "node", None),
        P("node", "dp"),
        P("node", None),
        P("node", None),
    )
    return jax.shard_map(
        body,
        mesh=mesh,
        in_specs=placed,
        out_specs=(P("dp", "node", None), P("dp", "node", None), P("node", "dp"), P()),
        check_vma=False,
    )
```

```python
import functools

import jax
import jax.numpy as jnp
from jax import lax
from jax.experimental import pallas as pl
from jax.experimental.pallas import tpu as pltpu
from jax.sharding import PartitionSpec as P

beta_one = 0.9
epsilon = 1e-06
learn_rate = 0.5
LANES = 128

VMEM = pl.BlockSpec(memory_space=pltpu.VMEM)
HBM = pl.BlockSpec(memory_space=pltpu.HBM)
MIB = 2**20


def near(*values):
    return [pltpu.with_memory_space_constraint(v, pltpu.VMEM) for v in values]


def far(*values):
    return [pltpu.with_memory_space_constraint(v, pltpu.HBM) for v in values]


def cut(cols):
    if cols % (3 * LANES):
        return [pl.ds(0, cols)]
    first = cols // 3 * 2
    return [pl.ds(0, first), pl.ds(first, cols - first)]


def gradient_kernel(
    cotan_hbm, momentum_hbm, master_hbm, second_hbm, acts_hbm,
    base_ref, theirs_ref, master_ref, bottom_ref,
    cotan_ref, acts, window, sems, cotan_sem, base_sem, master_sem, second_sem,
):
    rows = cotan_ref.shape[0]
    own = base_ref.shape[0]
    width, span, cols = master_ref.shape[1], window.shape[2], master_hbm.shape[1]
    column = lax.axis_index("dp") * width
    start = jnp.minimum((column // LANES) * LANES, cols - span)
    here = pl.ds(pl.multiple_of(start, LANES), span)
    spans = cut(cols)
    cotan_copy = pltpu.make_async_copy(cotan_hbm, cotan_ref, cotan_sem)
    master_copy = pltpu.make_async_copy(master_hbm.at[:, here], window.at[0], master_sem)
    second_copy = pltpu.make_async_copy(second_hbm.at[:, here], window.at[1], second_sem)
    base_copy = pltpu.make_async_copy(momentum_hbm, base_ref, base_sem)
    copies = [pltpu.make_async_copy(acts_hbm.at[:, s], acts.at[:, s], sems.at[i]) for i, s in enumerate(spans)]
    cotan_copy.start()
    copies[0].start()
    master_copy.start()
    second_copy.start()
    base_copy.start()
    for copy in copies[1:]:
        copy.start()
    shift = lax.rem(rows - lax.axis_index("node") * own, rows)
    cotan_copy.wait()
    cotan = pltpu.roll(cotan_ref[...].astype(jnp.float32), shift, 0).astype(jnp.bfloat16)
    shift = lax.rem(span - (column - start), span)
    master_copy.wait()
    second_copy.wait()
    master_ref[...] = pltpu.roll(window[0], shift, 1)[:, :width]
    bottom_ref[...] = jnp.sqrt(pltpu.roll(window[1], shift, 1)[:, :width]) + 1e-08
    for i, (copy, s) in enumerate(zip(copies, spans)):
        copy.wait()
        if i == 0:
            base_copy.wait()
        sums = jnp.dot(cotan, acts[:, s], preferred_element_type=jnp.float32)
        base_ref[:, s] = beta_one * base_ref[:, s] + (1.0 - beta_one) * sums[:own]
        for k in range(theirs_ref.shape[0]):
            theirs_ref[k, :, s] = sums[(k + 1) * own : (k + 2) * own]


def moment_of(base_ref, arrived_refs):
    rest = arrived_refs[0][...]
    for ref in arrived_refs[1:]:
        rest = rest + ref[...]
    return base_ref[...] + (1.0 - beta_one) * rest


def compress(values):
    scale = jnp.sqrt(jnp.mean(values * values, keepdims=True) + epsilon)
    return (scale * jnp.tanh(values / scale)).astype(jnp.bfloat16)


def send_kernel(order, error_ref, base_ref, *refs):
    arrived_refs, (blocks_ref, moment_ref, new_error_ref) = refs[:-3], refs[-3:]
    moment = moment_of(base_ref, arrived_refs)
    moment_ref[...] = moment
    carried = moment + error_ref[...]
    sent = compress(carried)
    new_error_ref[...] = carried - sent.astype(jnp.float32)
    width = blocks_ref.shape[2]
    for place, i in enumerate(order):
        blocks_ref[place] = sent[:, i * width : (i + 1) * width]


def serve_kernel(blocks_ref, error_ref, master_ref, bottom_ref, new_error_ref, out_ref):
    replicas = blocks_ref.shape[0]
    total = blocks_ref[0].astype(jnp.float32)
    for i in range(1, replicas):
        total = total + blocks_ref[i].astype(jnp.float32)
    served = total / replicas + error_ref[...]
    returned = compress(served).astype(jnp.float32)
    new_error_ref[...] = served - returned
    weights = (master_ref[...] - learn_rate * (returned / bottom_ref[...])).astype(jnp.bfloat16)
    for i in range(replicas):
        out_ref[i] = weights


def keep_kernel(*refs):
    *kept, _ = refs[: len(refs) // 2 + 1]
    for source, target in zip(kept, refs[len(kept) + 1 :]):
        target[...] = source[...]


def assemble_kernel(order, *refs):
    parts, (out_hbm, out, sems) = refs[:-3], refs[-3:]
    nodes = len(parts)
    servers, own, width = parts[0].shape
    groups = sems.shape[0]
    each = servers // groups
    me = lax.axis_index("node")
    copies = []
    for i in range(servers):
        loaded = [part[order.index(i)].astype(jnp.float32) for part in parts]
        stacked = []
        for node in range(nodes):
            chosen = loaded[0]
            for k in range(1, nodes):
                chosen = jnp.where(lax.rem(me - k + nodes, nodes) == node, loaded[k], chosen)
            stacked.append(chosen)
        out[:, i * width : (i + 1) * width] = jnp.concatenate(stacked, axis=0).astype(jnp.bfloat16)
        if (i + 1) % each == 0:
            group = i // each
            s = pl.ds(group * each * width, each * width)
            copies.append(pltpu.make_async_copy(out.at[:, s], out_hbm.at[:, s], sems.at[group]))
            copies[-1].start()
    for copy in copies:
        copy.wait()


def ordered(count):
    lead = count // 2 + count // 8
    return [(lead + i) % count for i in range(count)]


def body(hidden, cotangent, momentum, worker_error, server_error, master, second_moment):
    f32, bf16 = jnp.float32, jnp.bfloat16
    nodes, servers = lax.axis_size("node"), lax.axis_size("dp")
    tokens, cols = hidden.shape[1:]
    rows, own = cotangent.shape[2], momentum.shape[1]
    width = cols // servers
    shape = jax.ShapeDtypeStruct

    def exchange(blocks):
        return lax.all_to_all(blocks, "dp", split_axis=0, concat_axis=0, axis_index_groups=[order], tiled=True)

    order = ordered(servers)

    def turn(value, k):
        return lax.ppermute(value, "node", [(i, (i + k) % nodes) for i in range(nodes)])

    def call(kernel, name, outs, in_specs, scratch=(), out_specs=None):
        return pl.pallas_call(
            kernel,
            name=name,
            out_shape=outs,
            in_specs=in_specs,
            out_specs=out_specs or jax.tree.map(lambda _: VMEM, outs),
            scratch_shapes=scratch,
            compiler_params=pltpu.CompilerParams(vmem_limit_bytes=16 * MIB),
        )

    dma = pltpu.SemaphoreType.DMA
    span = min(cols, -(-width // LANES) * LANES + LANES)
    base, theirs, master_part, bottom = call(
        gradient_kernel,
        "gradient",
        (
            pltpu.VMEM((own, cols), f32),
            pltpu.VMEM((nodes - 1, own, cols), f32),
            pltpu.VMEM((own, width), f32),
            pltpu.VMEM((own, width), f32),
        ),
        [HBM] * 5,
        [pltpu.VMEM((rows, tokens), bf16), pltpu.VMEM((tokens, cols), bf16), pltpu.VMEM((2, own, span), f32)]
        + [dma((len(cut(cols)),))] + [dma(())] * 4,
    )(*far(cotangent[0].T, momentum[0], master, second_moment, hidden[0]))
    arrived = [turn(theirs[k - 1], k) for k in range(1, nodes)]

    blocks, moment, new_worker = call(
        functools.partial(send_kernel, order),
        "send",
        (pltpu.VMEM((servers, own, width), bf16), pltpu.VMEM((own, cols), f32), pltpu.VMEM((own, cols), f32)),
        [VMEM] * (2 + len(arrived)),
    )(*near(worker_error[0], base, *arrived))
    gathered = exchange(blocks)

    new_server, copies = call(
        serve_kernel,
        "serve",
        (pltpu.VMEM((own, width), f32), pltpu.VMEM((servers, own, width), bf16)),
        [VMEM] * 4,
    )(*near(gathered, server_error, master_part, bottom))
    everyone = exchange(copies)
    parts = [everyone] + [turn(everyone, k) for k in range(1, nodes)]

    kept = near(moment, new_worker, new_server, everyone)
    moment, new_worker, new_server = call(
        keep_kernel, "keep", tuple(shape(v.shape, f32) for v in kept[:3]), [VMEM] * 4
    )(*kept)

    groups = 2 if servers % 2 == 0 and cols % (2 * LANES) == 0 else 1
    weights = call(
        functools.partial(assemble_kernel, order),
        "assemble",
        shape((rows, cols), bf16),
        [VMEM] * nodes,
        [pltpu.VMEM((rows, cols), bf16), dma((groups,))],
        HBM,
    )(*near(*parts))
    return (moment[None], new_worker[None], new_server, weights)


def solution(mesh):
    placed = (
        P("dp", "node", None),
        P("dp", "node", None),
        P("dp", "node", None),
        P("dp", "node", None),
        P("node", "dp"),
        P("node", None),
        P("node", None),
    )
    return jax.shard_map(
        body,
        mesh=mesh,
        in_specs=placed,
        out_specs=(P("dp", "node", None), P("dp", "node", None), P("node", "dp"), P()),
        check_vma=False,
    )
```

```python
import functools

import jax
import jax.numpy as jnp
from jax import lax
from jax.experimental import pallas as pl
from jax.experimental.pallas import tpu as pltpu
from jax.sharding import PartitionSpec as P

beta_one = 0.9
epsilon = 1e-06
learn_rate = 0.5
LANES = 128

VMEM = pl.BlockSpec(memory_space=pltpu.VMEM)
HBM = pl.BlockSpec(memory_space=pltpu.HBM)
MIB = 2**20


def near(*values):
    return [pltpu.with_memory_space_constraint(v, pltpu.VMEM) for v in values]


def far(*values):
    return [pltpu.with_memory_space_constraint(v, pltpu.HBM) for v in values]


def cut(cols):
    if cols % (3 * LANES):
        return [pl.ds(0, cols)]
    first = cols // 3 * 2
    return [pl.ds(0, first), pl.ds(first, cols - first)]


def gradient_kernel(
    cotan_hbm, momentum_hbm, master_hbm, second_hbm, acts_hbm,
    base_ref, theirs_ref, master_ref, bottom_ref,
    cotan_ref, acts, window, sems, cotan_sem, base_sem, master_sem, second_sem,
):
    rows = cotan_ref.shape[0]
    own = base_ref.shape[0]
    width, span, cols = master_ref.shape[1], window.shape[2], master_hbm.shape[1]
    column = lax.axis_index("dp") * width
    start = jnp.minimum((column // LANES) * LANES, cols - span)
    here = pl.ds(pl.multiple_of(start, LANES), span)
    spans = cut(cols)
    cotan_copy = pltpu.make_async_copy(cotan_hbm, cotan_ref, cotan_sem)
    master_copy = pltpu.make_async_copy(master_hbm.at[:, here], window.at[0], master_sem)
    second_copy = pltpu.make_async_copy(second_hbm.at[:, here], window.at[1], second_sem)
    base_copy = pltpu.make_async_copy(momentum_hbm, base_ref, base_sem)
    copies = [pltpu.make_async_copy(acts_hbm.at[:, s], acts.at[:, s], sems.at[i]) for i, s in enumerate(spans)]
    cotan_copy.start()
    copies[0].start()
    master_copy.start()
    second_copy.start()
    base_copy.start()
    for copy in copies[1:]:
        copy.start()
    shift = lax.rem(rows - lax.axis_index("node") * own, rows)
    cotan_copy.wait()
    cotan = pltpu.roll(cotan_ref[...].astype(jnp.float32), shift, 0).astype(jnp.bfloat16)
    shift = lax.rem(span - (column - start), span)
    master_copy.wait()
    second_copy.wait()
    master_ref[...] = pltpu.roll(window[0], shift, 1)[:, :width]
    bottom_ref[...] = jnp.sqrt(pltpu.roll(window[1], shift, 1)[:, :width]) + 1e-08
    for i, (copy, s) in enumerate(zip(copies, spans)):
        copy.wait()
        if i == 0:
            base_copy.wait()
        sums = jnp.dot(cotan, acts[:, s], preferred_element_type=jnp.float32)
        base_ref[:, s] = beta_one * base_ref[:, s] + (1.0 - beta_one) * sums[:own]
        for k in range(theirs_ref.shape[0]):
            theirs_ref[k, :, s] = sums[(k + 1) * own : (k + 2) * own]


def moment_of(base_ref, arrived_refs):
    rest = arrived_refs[0][...]
    for ref in arrived_refs[1:]:
        rest = rest + ref[...]
    return base_ref[...] + (1.0 - beta_one) * rest


def compress(values):
    scale = jnp.sqrt(jnp.mean(values * values, keepdims=True) + epsilon)
    return (scale * jnp.tanh(values / scale)).astype(jnp.bfloat16)


def send_kernel(order, error_ref, base_ref, *refs):
    arrived_refs, (blocks_ref, moment_ref, new_error_ref) = refs[:-3], refs[-3:]
    moment = moment_of(base_ref, arrived_refs)
    moment_ref[...] = moment
    carried = moment + error_ref[...]
    sent = compress(carried)
    new_error_ref[...] = carried - sent.astype(jnp.float32)
    width = blocks_ref.shape[2]
    for place, i in enumerate(order):
        blocks_ref[place] = sent[:, i * width : (i + 1) * width]


def serve_kernel(blocks_ref, error_ref, master_ref, bottom_ref, new_error_ref, out_ref):
    replicas = blocks_ref.shape[0]
    total = blocks_ref[0].astype(jnp.float32)
    for i in range(1, replicas):
        total = total + blocks_ref[i].astype(jnp.float32)
    served = total / replicas + error_ref[...]
    returned = compress(served).astype(jnp.float32)
    new_error_ref[...] = served - returned
    weights = (master_ref[...] - learn_rate * (returned / bottom_ref[...])).astype(jnp.bfloat16)
    for i in range(replicas):
        out_ref[i] = weights


def lay_out(order, blocks_ref, rows_ref):
    width = blocks_ref.shape[2]
    for i in range(len(order)):
        rows_ref[:, i * width : (i + 1) * width] = blocks_ref[order.index(i)]


def keep_kernel(order, moment_ref, error_ref, server_ref, blocks_ref, moment_hbm, error_hbm, server_hbm, weights_hbm, rows, sems):
    pairs = [(moment_ref, moment_hbm), (error_ref, error_hbm), (server_ref, server_hbm)]
    copies = [pltpu.make_async_copy(source, target, sems.at[i]) for i, (source, target) in enumerate(pairs)]
    for copy in copies:
        copy.start()
    lay_out(order, blocks_ref, rows)
    copies.append(pltpu.make_async_copy(rows, weights_hbm.at[lax.axis_index("node")], sems.at[len(pairs)]))
    copies[-1].start()
    for copy in copies:
        copy.wait()


def assemble_kernel(order, *refs):
    *parts, _, out_hbm, rows, sems = refs
    nodes = out_hbm.shape[0]
    me = lax.axis_index("node")
    copies = []
    for k, part in enumerate(parts):
        lay_out(order, part, rows.at[k])
        sender = lax.rem(me - (k + 1) + nodes, nodes)
        copies.append(pltpu.make_async_copy(rows.at[k], out_hbm.at[sender], sems.at[k]))
        copies[-1].start()
    for copy in copies:
        copy.wait()


def ordered(count):
    lead = count // 2 + count // 4 - 1
    return [lead ^ i if count & (count - 1) == 0 else (lead - i) % count for i in range(count)]


def body(hidden, cotangent, momentum, worker_error, server_error, master, second_moment):
    f32, bf16 = jnp.float32, jnp.bfloat16
    nodes, servers = lax.axis_size("node"), lax.axis_size("dp")
    tokens, cols = hidden.shape[1:]
    rows, own = cotangent.shape[2], momentum.shape[1]
    width = cols // servers
    shape = jax.ShapeDtypeStruct

    def exchange(blocks):
        return lax.all_to_all(blocks, "dp", split_axis=0, concat_axis=0, axis_index_groups=[order], tiled=True)

    order = ordered(servers)

    def turn(value, k):
        return lax.ppermute(value, "node", [(i, (i + k) % nodes) for i in range(nodes)])

    def call(kernel, name, outs, in_specs, scratch=(), out_specs=None, aliases={}):
        return pl.pallas_call(
            kernel,
            name=name,
            out_shape=outs,
            in_specs=in_specs,
            out_specs=out_specs or jax.tree.map(lambda _: VMEM, outs),
            scratch_shapes=scratch,
            input_output_aliases=aliases,
            compiler_params=pltpu.CompilerParams(vmem_limit_bytes=16 * MIB),
        )

    dma = pltpu.SemaphoreType.DMA
    span = min(cols, -(-width // LANES) * LANES + LANES)
    base, theirs, master_part, bottom = call(
        gradient_kernel,
        "gradient",
        (
            pltpu.VMEM((own, cols), f32),
            pltpu.VMEM((nodes - 1, own, cols), f32),
            pltpu.VMEM((own, width), f32),
            pltpu.VMEM((own, width), f32),
        ),
        [HBM] * 5,
        [pltpu.VMEM((rows, tokens), bf16), pltpu.VMEM((tokens, cols), bf16), pltpu.VMEM((2, own, span), f32)]
        + [dma((len(cut(cols)),))] + [dma(())] * 4,
    )(*far(cotangent[0].T, momentum[0], master, second_moment, hidden[0]))
    arrived = [turn(theirs[k - 1], k) for k in range(1, nodes)]

    blocks, moment, new_worker = call(
        functools.partial(send_kernel, order),
        "send",
        (pltpu.VMEM((servers, own, width), bf16), pltpu.VMEM((own, cols), f32), pltpu.VMEM((own, cols), f32)),
        [VMEM] * (2 + len(arrived)),
    )(*near(worker_error[0], base, *arrived))
    gathered = exchange(blocks)

    new_server, copies = call(
        serve_kernel,
        "serve",
        (pltpu.VMEM((own, width), f32), pltpu.VMEM((servers, own, width), bf16)),
        [VMEM] * 4,
    )(*near(gathered, server_error, master_part, bottom))
    everyone = exchange(copies)
    others = [turn(everyone, k) for k in range(1, nodes)]

    whole = (nodes, own, cols)
    moment, new_worker, new_server, weights = call(
        functools.partial(keep_kernel, order),
        "keep",
        (*(shape(v.shape, f32) for v in (moment, new_worker, new_server)), shape(whole, bf16)),
        [VMEM] * 4,
        [pltpu.VMEM((own, cols), bf16), dma((4,))],
        (HBM,) * 4,
    )(*near(moment, new_worker, new_server, everyone))
    weights = call(
        functools.partial(assemble_kernel, order),
        "assemble",
        shape(whole, bf16),
        [VMEM] * len(others) + [HBM],
        [pltpu.VMEM((nodes - 1, own, cols), bf16), dma((nodes - 1,))],
        HBM,
        {len(others): 0},
    )(*near(*others), weights)
    weights = weights.reshape(rows, cols)
    return (moment[None], new_worker[None], new_server, weights)


def solution(mesh):
    placed = (
        P("dp", "node", None),
        P("dp", "node", None),
        P("dp", "node", None),
        P("dp", "node", None),
        P("node", "dp"),
        P("node", None),
        P("node", None),
    )
    return jax.shard_map(
        body,
        mesh=mesh,
        in_specs=placed,
        out_specs=(P("dp", "node", None), P("dp", "node", None), P("node", "dp"), P()),
        check_vma=False,
    )
```

```python
import functools

import jax
import jax.numpy as jnp
from jax import lax
from jax.experimental import pallas as pl
from jax.experimental.pallas import tpu as pltpu
from jax.sharding import PartitionSpec as P

beta_one = 0.9
epsilon = 1e-06
learn_rate = 0.5
LANES = 128

VMEM = pl.BlockSpec(memory_space=pltpu.VMEM)
HBM = pl.BlockSpec(memory_space=pltpu.HBM)
MIB = 2**20


def near(*values):
    return [pltpu.with_memory_space_constraint(v, pltpu.VMEM) for v in values]


def far(*values):
    return [pltpu.with_memory_space_constraint(v, pltpu.HBM) for v in values]


def cut(cols):
    if cols % (3 * LANES):
        return [pl.ds(0, cols)]
    first = cols // 3 * 2
    return [pl.ds(0, first), pl.ds(first, cols - first)]


def gradient_kernel(cotan_hbm, acts_hbm, mine_ref, theirs_ref, cotan_ref, acts, cotan_sem, sems):
    rows = cotan_ref.shape[0]
    own = mine_ref.shape[0]
    spans = cut(acts.shape[1])
    cotan_copy = pltpu.make_async_copy(cotan_hbm, cotan_ref, cotan_sem)
    copies = [pltpu.make_async_copy(acts_hbm.at[:, s], acts.at[:, s], sems.at[i]) for i, s in enumerate(spans)]
    for copy in [cotan_copy, *copies]:
        copy.start()
    shift = lax.rem(rows - lax.axis_index("node") * own, rows)
    cotan_copy.wait()
    cotan = pltpu.roll(cotan_ref[...].astype(jnp.float32), shift, 0).astype(jnp.bfloat16)
    for copy, s in zip(copies, spans):
        copy.wait()
        sums = jnp.dot(cotan, acts[:, s], preferred_element_type=jnp.float32)
        mine_ref[:, s] = sums[:own]
        for k in range(theirs_ref.shape[0]):
            theirs_ref[k, :, s] = sums[(k + 1) * own : (k + 2) * own]


def prepare_kernel(
    momentum_hbm, error_hbm, server_hbm, master_hbm, second_hbm, mine_ref,
    base_ref, error_ref, server_ref, master_ref, bottom_ref, window, sems,
):
    width, span, cols = master_ref.shape[1], window.shape[2], master_hbm.shape[1]
    column = lax.axis_index("dp") * width
    start = jnp.minimum((column // LANES) * LANES, cols - span)
    here = pl.ds(pl.multiple_of(start, LANES), span)
    pairs = [
        (master_hbm.at[:, here], window.at[0]),
        (second_hbm.at[:, here], window.at[1]),
        (server_hbm, server_ref),
        (momentum_hbm, base_ref),
        (error_hbm, error_ref),
    ]
    copies = [pltpu.make_async_copy(source, target, sems.at[i]) for i, (source, target) in enumerate(pairs)]
    for copy in copies:
        copy.start()
    shift = lax.rem(span - (column - start), span)
    copies[0].wait()
    copies[1].wait()
    master_ref[...] = pltpu.roll(window[0], shift, 1)[:, :width]
    bottom_ref[...] = jnp.sqrt(pltpu.roll(window[1], shift, 1)[:, :width]) + 1e-08
    for copy in copies[2:4]:
        copy.wait()
    base_ref[...] = beta_one * base_ref[...] + (1.0 - beta_one) * mine_ref[...]
    copies[4].wait()


def moment_of(base_ref, arrived_refs):
    rest = arrived_refs[0][...]
    for ref in arrived_refs[1:]:
        rest = rest + ref[...]
    return base_ref[...] + (1.0 - beta_one) * rest


def compress(values):
    scale = jnp.sqrt(jnp.mean(values * values, keepdims=True) + epsilon)
    return (scale * jnp.tanh(values / scale)).astype(jnp.bfloat16)


def send_kernel(order, error_ref, base_ref, *refs):
    arrived_refs, (blocks_ref, moment_ref, new_error_ref) = refs[:-3], refs[-3:]
    moment = moment_of(base_ref, arrived_refs)
    moment_ref[...] = moment
    carried = moment + error_ref[...]
    sent = compress(carried)
    new_error_ref[...] = carried - sent.astype(jnp.float32)
    width = blocks_ref.shape[2]
    for place, i in enumerate(order):
        blocks_ref[place] = sent[:, i * width : (i + 1) * width]


def serve_kernel(blocks_ref, error_ref, master_ref, bottom_ref, new_error_ref, out_ref):
    replicas = blocks_ref.shape[0]
    total = blocks_ref[0].astype(jnp.float32)
    for i in range(1, replicas):
        total = total + blocks_ref[i].astype(jnp.float32)
    served = total / replicas + error_ref[...]
    returned = compress(served).astype(jnp.float32)
    new_error_ref[...] = served - returned
    weights = (master_ref[...] - learn_rate * (returned / bottom_ref[...])).astype(jnp.bfloat16)
    for i in range(replicas):
        out_ref[i] = weights


def lay_out(order, blocks_ref, rows_ref):
    width = blocks_ref.shape[2]
    for i in range(len(order)):
        rows_ref[:, i * width : (i + 1) * width] = blocks_ref[order.index(i)]


def keep_kernel(order, moment_ref, error_ref, server_ref, blocks_ref, moment_hbm, error_hbm, server_hbm, weights_hbm, rows, sems):
    pairs = [(moment_ref, moment_hbm), (error_ref, error_hbm), (server_ref, server_hbm)]
    copies = [pltpu.make_async_copy(source, target, sems.at[i]) for i, (source, target) in enumerate(pairs)]
    for copy in copies:
        copy.start()
    lay_out(order, blocks_ref, rows)
    copies.append(pltpu.make_async_copy(rows, weights_hbm.at[lax.axis_index("node")], sems.at[len(pairs)]))
    copies[-1].start()
    for copy in copies:
        copy.wait()


def assemble_kernel(order, *refs):
    *parts, _, out_hbm, rows, sems = refs
    nodes = out_hbm.shape[0]
    me = lax.axis_index("node")
    copies = []
    for k, part in enumerate(parts):
        lay_out(order, part, rows.at[k])
        sender = lax.rem(me - (k + 1) + nodes, nodes)
        copies.append(pltpu.make_async_copy(rows.at[k], out_hbm.at[sender], sems.at[k]))
        copies[-1].start()
    for copy in copies:
        copy.wait()


def ordered(count):
    lead = count // 2 + count // 4 - 1
    return [lead ^ i if count & (count - 1) == 0 else (lead - i) % count for i in range(count)]


def body(hidden, cotangent, momentum, worker_error, server_error, master, second_moment):
    f32, bf16 = jnp.float32, jnp.bfloat16
    nodes, servers = lax.axis_size("node"), lax.axis_size("dp")
    tokens, cols = hidden.shape[1:]
    rows, own = cotangent.shape[2], momentum.shape[1]
    width = cols // servers
    shape = jax.ShapeDtypeStruct

    def exchange(blocks):
        return lax.all_to_all(blocks, "dp", split_axis=0, concat_axis=0, axis_index_groups=[order], tiled=True)

    order = ordered(servers)

    def turn(value, k):
        return lax.ppermute(value, "node", [(i, (i + k) % nodes) for i in range(nodes)])

    def call(kernel, name, outs, in_specs, scratch=(), out_specs=None, aliases={}):
        return pl.pallas_call(
            kernel,
            name=name,
            out_shape=outs,
            in_specs=in_specs,
            out_specs=out_specs or jax.tree.map(lambda _: VMEM, outs),
            scratch_shapes=scratch,
            input_output_aliases=aliases,
            compiler_params=pltpu.CompilerParams(vmem_limit_bytes=16 * MIB),
        )

    dma = pltpu.SemaphoreType.DMA
    mine, theirs = call(
        gradient_kernel,
        "gradient",
        (pltpu.VMEM((own, cols), f32), pltpu.VMEM((nodes - 1, own, cols), f32)),
        [HBM] * 2,
        [pltpu.VMEM((rows, tokens), bf16), pltpu.VMEM((tokens, cols), bf16), dma(()), dma((len(cut(cols)),))],
    )(*far(cotangent[0].T, hidden[0]))
    arrived = [turn(theirs[k - 1], k) for k in range(1, nodes)]

    span = min(cols, -(-width // LANES) * LANES + LANES)
    base, error, server, master_part, bottom = call(
        prepare_kernel,
        "prepare",
        (pltpu.VMEM((own, cols), f32),) * 2 + (pltpu.VMEM((own, width), f32),) * 3,
        [HBM] * 5 + [VMEM],
        [pltpu.VMEM((2, own, span), f32), dma((5,))],
    )(*far(momentum[0], worker_error[0], server_error, master, second_moment), *near(mine))

    blocks, moment, new_worker = call(
        functools.partial(send_kernel, order),
        "send",
        (pltpu.VMEM((servers, own, width), bf16), pltpu.VMEM((own, cols), f32), pltpu.VMEM((own, cols), f32)),
        [VMEM] * (2 + len(arrived)),
    )(*near(error, base, *arrived))
    gathered = exchange(blocks)

    new_server, copies = call(
        serve_kernel,
        "serve",
        (pltpu.VMEM((own, width), f32), pltpu.VMEM((servers, own, width), bf16)),
        [VMEM] * 4,
    )(*near(gathered, server, master_part, bottom))
    everyone = exchange(copies)
    others = [turn(everyone, k) for k in range(1, nodes)]

    whole = (nodes, own, cols)
    moment, new_worker, new_server, weights = call(
        functools.partial(keep_kernel, order),
        "keep",
        (*(shape(v.shape, f32) for v in (moment, new_worker, new_server)), shape(whole, bf16)),
        [VMEM] * 4,
        [pltpu.VMEM((own, cols), bf16), dma((4,))],
        (HBM,) * 4,
    )(*near(moment, new_worker, new_server, everyone))
    weights = call(
        functools.partial(assemble_kernel, order),
        "assemble",
        shape(whole, bf16),
        [VMEM] * len(others) + [HBM],
        [pltpu.VMEM((nodes - 1, own, cols), bf16), dma((nodes - 1,))],
        HBM,
        {len(others): 0},
    )(*near(*others), weights)
    weights = weights.reshape(rows, cols)
    return (moment[None], new_worker[None], new_server, weights)


def solution(mesh):
    placed = (
        P("dp", "node", None),
        P("dp", "node", None),
        P("dp", "node", None),
        P("dp", "node", None),
        P("node", "dp"),
        P("node", None),
        P("node", None),
    )
    return jax.shard_map(
        body,
        mesh=mesh,
        in_specs=placed,
        out_specs=(P("dp", "node", None), P("dp", "node", None), P("node", "dp"), P()),
        check_vma=False,
    )
```

```python
import functools

import jax
import jax.numpy as jnp
from jax import lax
from jax.experimental import pallas as pl
from jax.experimental.pallas import tpu as pltpu
from jax.sharding import PartitionSpec as P

beta_one = 0.9
epsilon = 1e-06
learn_rate = 0.5
LANES = 128

VMEM = pl.BlockSpec(memory_space=pltpu.VMEM)
HBM = pl.BlockSpec(memory_space=pltpu.HBM)
MIB = 2**20


def near(*values):
    return [pltpu.with_memory_space_constraint(v, pltpu.VMEM) for v in values]


def far(*values):
    return [pltpu.with_memory_space_constraint(v, pltpu.HBM) for v in values]


def cut(cols):
    if cols % (3 * LANES):
        return [pl.ds(0, cols)]
    first = cols // 3 * 2
    return [pl.ds(0, first), pl.ds(first, cols - first)]


def gradient_kernel(cotan_hbm, acts_hbm, mine_ref, theirs_ref, cotan_ref, acts, cotan_sem, sems):
    rows = cotan_ref.shape[0]
    own = mine_ref.shape[0]
    spans = cut(acts.shape[1])
    cotan_copy = pltpu.make_async_copy(cotan_hbm, cotan_ref, cotan_sem)
    copies = [pltpu.make_async_copy(acts_hbm.at[:, s], acts.at[:, s], sems.at[i]) for i, s in enumerate(spans)]
    for copy in [cotan_copy, *copies]:
        copy.start()
    shift = lax.rem(rows - lax.axis_index("node") * own, rows)
    cotan_copy.wait()
    cotan = pltpu.roll(cotan_ref[...].astype(jnp.float32), shift, 0).astype(jnp.bfloat16)
    for copy, s in zip(copies, spans):
        copy.wait()
        sums = jnp.dot(cotan, acts[:, s], preferred_element_type=jnp.float32)
        mine_ref[:, s] = sums[:own]
        for k in range(theirs_ref.shape[0]):
            theirs_ref[k, :, s] = sums[(k + 1) * own : (k + 2) * own]


def prepare_kernel(
    momentum_hbm, error_hbm, server_hbm, master_hbm, second_hbm, mine_ref,
    base_ref, start_ref, server_ref, master_ref, bottom_ref, window, sems,
):
    width, span, cols = master_ref.shape[1], window.shape[2], master_hbm.shape[1]
    column = lax.axis_index("dp") * width
    start = jnp.minimum((column // LANES) * LANES, cols - span)
    here = pl.ds(pl.multiple_of(start, LANES), span)
    pairs = [
        (master_hbm.at[:, here], window.at[0]),
        (second_hbm.at[:, here], window.at[1]),
        (server_hbm, server_ref),
        (momentum_hbm, base_ref),
        (error_hbm, start_ref),
    ]
    copies = [pltpu.make_async_copy(source, target, sems.at[i]) for i, (source, target) in enumerate(pairs)]
    for copy in copies:
        copy.start()
    shift = lax.rem(span - (column - start), span)
    copies[0].wait()
    copies[1].wait()
    master_ref[...] = pltpu.roll(window[0], shift, 1)[:, :width]
    bottom_ref[...] = jnp.sqrt(pltpu.roll(window[1], shift, 1)[:, :width]) + 1e-08
    for copy in copies[2:4]:
        copy.wait()
    base = beta_one * base_ref[...] + (1.0 - beta_one) * mine_ref[...]
    base_ref[...] = base
    copies[4].wait()
    start_ref[...] = base + start_ref[...]


def arrived_part(arrived_refs, s):
    rest = arrived_refs[0][:, s]
    for ref in arrived_refs[1:]:
        rest = rest + ref[:, s]
    return (1.0 - beta_one) * rest


def compress(values, squares):
    scale = jnp.sqrt(squares + epsilon)
    return (scale * jnp.tanh(values / scale)).astype(jnp.bfloat16)


def send_kernel(order, start_ref, *refs):
    arrived_refs, (blocks_ref, sent_ref) = refs[:-2], refs[-2:]
    rows, cols = start_ref.shape
    width = blocks_ref.shape[2]
    chunks = piece_count(len(order), width)
    step = cols // chunks

    def squares(i, total):
        s = pl.ds(pl.multiple_of(i * step, LANES), step)
        carried = start_ref[:, s] + arrived_part(arrived_refs, s)
        return total + carried * carried

    total = lax.fori_loop(0, chunks, squares, jnp.zeros((rows, step), jnp.float32))
    mean = jnp.sum(total, keepdims=True) / (rows * cols)
    sent = compress(start_ref[...] + arrived_part(arrived_refs, slice(None)), mean)
    sent_ref[...] = sent
    for place, i in enumerate(order):
        blocks_ref[place] = sent[:, i * width : (i + 1) * width]


def serve_kernel(blocks_ref, error_ref, master_ref, bottom_ref, new_error_ref, out_ref):
    replicas = blocks_ref.shape[0]
    total = blocks_ref[0].astype(jnp.float32)
    for i in range(1, replicas):
        total = total + blocks_ref[i].astype(jnp.float32)
    served = total / replicas + error_ref[...]
    returned = compress(served, jnp.mean(served * served, keepdims=True)).astype(jnp.float32)
    new_error_ref[...] = served - returned
    weights = (master_ref[...] - learn_rate * (returned / bottom_ref[...])).astype(jnp.bfloat16)
    for i in range(replicas):
        out_ref[i] = weights


def lay_out(order, blocks_ref, rows_ref):
    width = blocks_ref.shape[2]
    for i in range(len(order)):
        rows_ref[:, i * width : (i + 1) * width] = blocks_ref[order.index(i)]


def piece_count(servers, width):
    return max(n for n in (1, 2, 4) if servers % n == 0 and servers // n * width % LANES == 0)


def keep_kernel(order, base_ref, start_ref, sent_ref, server_ref, blocks_ref, *refs):
    *arrived_refs, moment_hbm, error_hbm, server_hbm, weights_hbm, moment, error, rows, sems = refs
    copies = [
        pltpu.make_async_copy(server_ref, server_hbm, sems.at[0]),
        pltpu.make_async_copy(moment, moment_hbm, sems.at[1]),
        pltpu.make_async_copy(error, error_hbm, sems.at[2]),
        pltpu.make_async_copy(rows, weights_hbm.at[lax.axis_index("node")], sems.at[3]),
    ]
    copies[0].start()
    rest = arrived_part(arrived_refs, slice(None))
    moment[...] = base_ref[...] + rest
    copies[1].start()
    error[...] = (start_ref[...] + rest) - sent_ref[...].astype(jnp.float32)
    copies[2].start()
    lay_out(order, blocks_ref, rows)
    copies[3].start()
    for copy in copies:
        copy.wait()


def assemble_kernel(order, *refs):
    *parts, _, out_hbm, rows, sems = refs
    nodes = out_hbm.shape[0]
    me = lax.axis_index("node")
    copies = []
    for k, part in enumerate(parts):
        lay_out(order, part, rows.at[k])
        sender = lax.rem(me - (k + 1) + nodes, nodes)
        copies.append(pltpu.make_async_copy(rows.at[k], out_hbm.at[sender], sems.at[k]))
        copies[-1].start()
    for copy in copies:
        copy.wait()


def ordered(count):
    lead = count // 2 + count // 4 - 1
    return [lead ^ i if count & (count - 1) == 0 else (lead - i) % count for i in range(count)]


def body(hidden, cotangent, momentum, worker_error, server_error, master, second_moment):
    f32, bf16 = jnp.float32, jnp.bfloat16
    nodes, servers = lax.axis_size("node"), lax.axis_size("dp")
    tokens, cols = hidden.shape[1:]
    rows, own = cotangent.shape[2], momentum.shape[1]
    width = cols // servers
    shape = jax.ShapeDtypeStruct

    def exchange(blocks):
        return lax.all_to_all(blocks, "dp", split_axis=0, concat_axis=0, axis_index_groups=[order], tiled=True)

    order = ordered(servers)

    def turn(value, k):
        return lax.ppermute(value, "node", [(i, (i + k) % nodes) for i in range(nodes)])

    def call(kernel, name, outs, in_specs, scratch=(), out_specs=None, aliases={}):
        return pl.pallas_call(
            kernel,
            name=name,
            out_shape=outs,
            in_specs=in_specs,
            out_specs=out_specs or jax.tree.map(lambda _: VMEM, outs),
            scratch_shapes=scratch,
            input_output_aliases=aliases,
            compiler_params=pltpu.CompilerParams(vmem_limit_bytes=16 * MIB),
        )

    dma = pltpu.SemaphoreType.DMA
    mine, theirs = call(
        gradient_kernel,
        "gradient",
        (pltpu.VMEM((own, cols), f32), pltpu.VMEM((nodes - 1, own, cols), f32)),
        [HBM] * 2,
        [pltpu.VMEM((rows, tokens), bf16), pltpu.VMEM((tokens, cols), bf16), dma(()), dma((len(cut(cols)),))],
    )(*far(cotangent[0].T, hidden[0]))
    arrived = [turn(theirs[k - 1], k) for k in range(1, nodes)]

    span = min(cols, -(-width // LANES) * LANES + LANES)
    base, begun, server, master_part, bottom = call(
        prepare_kernel,
        "prepare",
        (pltpu.VMEM((own, cols), f32),) * 2 + (pltpu.VMEM((own, width), f32),) * 3,
        [HBM] * 5 + [VMEM],
        [pltpu.VMEM((2, own, span), f32), dma((5,))],
    )(*far(momentum[0], worker_error[0], server_error, master, second_moment), *near(mine))

    blocks, sent = call(
        functools.partial(send_kernel, order),
        "send",
        (pltpu.VMEM((servers, own, width), bf16), pltpu.VMEM((own, cols), bf16)),
        [VMEM] * (1 + len(arrived)),
    )(*near(begun, *arrived))
    gathered = exchange(blocks)

    new_server, copies = call(
        serve_kernel,
        "serve",
        (pltpu.VMEM((own, width), f32), pltpu.VMEM((servers, own, width), bf16)),
        [VMEM] * 4,
    )(*near(gathered, server, master_part, bottom))
    everyone = exchange(copies)
    others = [turn(everyone, k) for k in range(1, nodes)]

    whole = (nodes, own, cols)
    moment, new_worker, new_server, weights = call(
        functools.partial(keep_kernel, order),
        "keep",
        (shape((own, cols), f32), shape((own, cols), f32), shape((own, width), f32), shape(whole, bf16)),
        [VMEM] * (5 + len(arrived)),
        [pltpu.VMEM((own, cols), f32)] * 2 + [pltpu.VMEM((own, cols), bf16), dma((4,))],
        (HBM,) * 4,
    )(*near(base, begun, sent, new_server, everyone, *arrived))
    weights = call(
        functools.partial(assemble_kernel, order),
        "assemble",
        shape(whole, bf16),
        [VMEM] * len(others) + [HBM],
        [pltpu.VMEM((nodes - 1, own, cols), bf16), dma((nodes - 1,))],
        HBM,
        {len(others): 0},
    )(*near(*others), weights)
    weights = weights.reshape(rows, cols)
    return (moment[None], new_worker[None], new_server, weights)


def solution(mesh):
    placed = (
        P("dp", "node", None),
        P("dp", "node", None),
        P("dp", "node", None),
        P("dp", "node", None),
        P("node", "dp"),
        P("node", None),
        P("node", None),
    )
    return jax.shard_map(
        body,
        mesh=mesh,
        in_specs=placed,
        out_specs=(P("dp", "node", None), P("dp", "node", None), P("node", "dp"), P()),
        check_vma=False,
    )
```

```python
import functools

import jax
import jax.numpy as jnp
from jax import lax
from jax.experimental import pallas as pl
from jax.experimental.pallas import tpu as pltpu
from jax.sharding import PartitionSpec as P

beta_one = 0.9
epsilon = 1e-06
learn_rate = 0.5
LANES = 128

VMEM = pl.BlockSpec(memory_space=pltpu.VMEM)
HBM = pl.BlockSpec(memory_space=pltpu.HBM)
MIB = 2**20


def near(*values):
    return [pltpu.with_memory_space_constraint(v, pltpu.VMEM) for v in values]


def far(*values):
    return [pltpu.with_memory_space_constraint(v, pltpu.HBM) for v in values]


def cut(cols):
    if cols % (3 * LANES):
        return [pl.ds(0, cols)]
    first = cols // 3 * 2
    return [pl.ds(0, first), pl.ds(first, cols - first)]


def gradient_kernel(cotan_hbm, acts_hbm, mine_ref, theirs_ref, cotan_ref, acts, cotan_sem, sems):
    rows = cotan_ref.shape[0]
    own = mine_ref.shape[0]
    spans = cut(acts.shape[1])
    cotan_copy = pltpu.make_async_copy(cotan_hbm, cotan_ref, cotan_sem)
    copies = [pltpu.make_async_copy(acts_hbm.at[:, s], acts.at[:, s], sems.at[i]) for i, s in enumerate(spans)]
    for copy in [cotan_copy, *copies]:
        copy.start()
    shift = lax.rem(rows - lax.axis_index("node") * own, rows)
    cotan_copy.wait()
    cotan = pltpu.roll(cotan_ref[...].astype(jnp.float32), shift, 0).astype(jnp.bfloat16)
    for copy, s in zip(copies, spans):
        copy.wait()
        sums = jnp.dot(cotan, acts[:, s], preferred_element_type=jnp.float32)
        mine_ref[:, s] = sums[:own]
        for k in range(theirs_ref.shape[0]):
            theirs_ref[k, :, s] = sums[(k + 1) * own : (k + 2) * own]


def prepare_kernel(
    momentum_hbm, error_hbm, server_hbm, master_hbm, second_hbm, mine_ref,
    base_ref, start_ref, server_ref, master_ref, bottom_ref, window, sems,
):
    width, span, cols = master_ref.shape[1], window.shape[2], master_hbm.shape[1]
    column = lax.axis_index("dp") * width
    start = jnp.minimum((column // LANES) * LANES, cols - span)
    here = pl.ds(pl.multiple_of(start, LANES), span)
    pairs = [
        (master_hbm.at[:, here], window.at[0]),
        (second_hbm.at[:, here], window.at[1]),
        (server_hbm, server_ref),
        (momentum_hbm, base_ref),
        (error_hbm, start_ref),
    ]
    copies = [pltpu.make_async_copy(source, target, sems.at[i]) for i, (source, target) in enumerate(pairs)]
    for copy in copies:
        copy.start()
    shift = lax.rem(span - (column - start), span)
    copies[0].wait()
    copies[1].wait()
    master_ref[...] = pltpu.roll(window[0], shift, 1)[:, :width]
    bottom_ref[...] = jnp.sqrt(pltpu.roll(window[1], shift, 1)[:, :width]) + 1e-08
    for copy in copies[2:4]:
        copy.wait()
    base = beta_one * base_ref[...] + (1.0 - beta_one) * mine_ref[...]
    base_ref[...] = base
    copies[4].wait()
    start_ref[...] = base + start_ref[...]


def arrived_part(arrived_refs, s):
    rest = arrived_refs[0][:, s]
    for ref in arrived_refs[1:]:
        rest = rest + ref[:, s]
    return (1.0 - beta_one) * rest


def compress(values, squares):
    scale = jnp.sqrt(squares + epsilon)
    return (scale * jnp.tanh(values / scale)).astype(jnp.bfloat16)


def send_kernel(order, start_ref, *refs):
    arrived_refs, (blocks_ref, sent_ref) = refs[:-2], refs[-2:]
    rows, cols = start_ref.shape
    width = blocks_ref.shape[2]
    chunks = piece_count(len(order), width)
    step = cols // chunks

    def squares(i, total):
        s = pl.ds(pl.multiple_of(i * step, LANES), step)
        carried = start_ref[:, s] + arrived_part(arrived_refs, s)
        return total + carried * carried

    total = lax.fori_loop(0, chunks, squares, jnp.zeros((rows, step), jnp.float32))
    mean = jnp.sum(total, keepdims=True) / (rows * cols)
    sent = compress(start_ref[...] + arrived_part(arrived_refs, slice(None)), mean)
    sent_ref[...] = sent
    for place, i in enumerate(order):
        blocks_ref[place] = sent[:, i * width : (i + 1) * width]


def serve_kernel(blocks_ref, error_ref, master_ref, bottom_ref, new_error_ref, out_ref):
    replicas = blocks_ref.shape[0]
    total = blocks_ref[0].astype(jnp.float32)
    for i in range(1, replicas):
        total = total + blocks_ref[i].astype(jnp.float32)
    served = total / replicas + error_ref[...]
    returned = compress(served, jnp.mean(served * served, keepdims=True)).astype(jnp.float32)
    new_error_ref[...] = served - returned
    weights = (master_ref[...] - learn_rate * (returned / bottom_ref[...])).astype(jnp.bfloat16)
    for i in range(replicas):
        out_ref[i] = weights


def lay_out(order, blocks_ref, rows_ref):
    width = blocks_ref.shape[2]
    for i in range(len(order)):
        rows_ref[:, i * width : (i + 1) * width] = blocks_ref[order.index(i)]


def piece_count(servers, width):
    return max(n for n in (1, 2, 4) if servers % n == 0 and servers // n * width % LANES == 0)


def keep_kernel(order, base_ref, start_ref, sent_ref, server_ref, blocks_ref, *refs):
    *arrived_refs, moment_hbm, error_hbm, server_hbm, weights_hbm, moment, error, rows, sems = refs
    copies = [
        pltpu.make_async_copy(server_ref, server_hbm, sems.at[0]),
        pltpu.make_async_copy(moment, moment_hbm, sems.at[1]),
        pltpu.make_async_copy(error, error_hbm, sems.at[2]),
        pltpu.make_async_copy(rows, weights_hbm.at[lax.axis_index("node")], sems.at[3]),
    ]
    copies[0].start()
    rest = arrived_part(arrived_refs, slice(None))
    moment[...] = base_ref[...] + rest
    copies[1].start()
    error[...] = (start_ref[...] + rest) - sent_ref[...].astype(jnp.float32)
    copies[2].start()
    lay_out(order, blocks_ref, rows)
    copies[3].start()
    for copy in copies:
        copy.wait()


def assemble_kernel(order, *refs):
    *parts, _, out_hbm, rows, sems = refs
    nodes = out_hbm.shape[0]
    me = lax.axis_index("node")
    copies = []
    for k, part in enumerate(parts):
        lay_out(order, part, rows.at[k])
        sender = lax.rem(me - (k + 1) + nodes, nodes)
        copies.append(pltpu.make_async_copy(rows.at[k], out_hbm.at[sender], sems.at[k]))
        copies[-1].start()
    for copy in copies:
        copy.wait()


def ordered(count, turned=False):
    lead = count // 2 + count // 4 - 1
    if count & (count - 1):
        return [(lead - i) % count for i in range(count)]
    bits = count.bit_length() - 1
    places = [sum((i >> k & 1) << (bits - 1 - k) for k in range(bits)) if turned else i for i in range(count)]
    return [lead ^ place for place in places]


def body(hidden, cotangent, momentum, worker_error, server_error, master, second_moment):
    f32, bf16 = jnp.float32, jnp.bfloat16
    nodes, servers = lax.axis_size("node"), lax.axis_size("dp")
    tokens, cols = hidden.shape[1:]
    rows, own = cotangent.shape[2], momentum.shape[1]
    width = cols // servers
    shape = jax.ShapeDtypeStruct

    def exchange(blocks, order):
        return lax.all_to_all(blocks, "dp", split_axis=0, concat_axis=0, axis_index_groups=[order], tiled=True)

    first, order = ordered(servers, True), ordered(servers)

    def turn(value, k):
        return lax.ppermute(value, "node", [(i, (i + k) % nodes) for i in range(nodes)])

    def call(kernel, name, outs, in_specs, scratch=(), out_specs=None, aliases={}):
        return pl.pallas_call(
            kernel,
            name=name,
            out_shape=outs,
            in_specs=in_specs,
            out_specs=out_specs or jax.tree.map(lambda _: VMEM, outs),
            scratch_shapes=scratch,
            input_output_aliases=aliases,
            compiler_params=pltpu.CompilerParams(vmem_limit_bytes=16 * MIB),
        )

    dma = pltpu.SemaphoreType.DMA
    mine, theirs = call(
        gradient_kernel,
        "gradient",
        (pltpu.VMEM((own, cols), f32), pltpu.VMEM((nodes - 1, own, cols), f32)),
        [HBM] * 2,
        [pltpu.VMEM((rows, tokens), bf16), pltpu.VMEM((tokens, cols), bf16), dma(()), dma((len(cut(cols)),))],
    )(*far(cotangent[0].T, hidden[0]))
    arrived = [turn(theirs[k - 1], k) for k in range(1, nodes)]

    span = min(cols, -(-width // LANES) * LANES + LANES)
    base, begun, server, master_part, bottom = call(
        prepare_kernel,
        "prepare",
        (pltpu.VMEM((own, cols), f32),) * 2 + (pltpu.VMEM((own, width), f32),) * 3,
        [HBM] * 5 + [VMEM],
        [pltpu.VMEM((2, own, span), f32), dma((5,))],
    )(*far(momentum[0], worker_error[0], server_error, master, second_moment), *near(mine))

    blocks, sent = call(
        functools.partial(send_kernel, first),
        "send",
        (pltpu.VMEM((servers, own, width), bf16), pltpu.VMEM((own, cols), bf16)),
        [VMEM] * (1 + len(arrived)),
    )(*near(begun, *arrived))
    gathered = exchange(blocks, first)

    new_server, copies = call(
        serve_kernel,
        "serve",
        (pltpu.VMEM((own, width), f32), pltpu.VMEM((servers, own, width), bf16)),
        [VMEM] * 4,
    )(*near(gathered, server, master_part, bottom))
    everyone = exchange(copies, order)
    others = [turn(everyone, k) for k in range(1, nodes)]

    whole = (nodes, own, cols)
    moment, new_worker, new_server, weights = call(
        functools.partial(keep_kernel, order),
        "keep",
        (shape((own, cols), f32), shape((own, cols), f32), shape((own, width), f32), shape(whole, bf16)),
        [VMEM] * (5 + len(arrived)),
        [pltpu.VMEM((own, cols), f32)] * 2 + [pltpu.VMEM((own, cols), bf16), dma((4,))],
        (HBM,) * 4,
    )(*near(base, begun, sent, new_server, everyone, *arrived))
    weights = call(
        functools.partial(assemble_kernel, order),
        "assemble",
        shape(whole, bf16),
        [VMEM] * len(others) + [HBM],
        [pltpu.VMEM((nodes - 1, own, cols), bf16), dma((nodes - 1,))],
        HBM,
        {len(others): 0},
    )(*near(*others), weights)
    weights = weights.reshape(rows, cols)
    return (moment[None], new_worker[None], new_server, weights)


def solution(mesh):
    placed = (
        P("dp", "node", None),
        P("dp", "node", None),
        P("dp", "node", None),
        P("dp", "node", None),
        P("node", "dp"),
        P("node", None),
        P("node", None),
    )
    return jax.shard_map(
        body,
        mesh=mesh,
        in_specs=placed,
        out_specs=(P("dp", "node", None), P("dp", "node", None), P("node", "dp"), P()),
        check_vma=False,
    )
```
